32 devices in a mesh: group: 2 (over x), wide: 2 (over core), tensor: 8 (over z, y).
Axes of the slice: x: 2, y: 2, z: 4, core: 2. Of those that a mesh axis runs over, the one named last changes fastest.
Arguments:
- tokens: bfloat16 [512, 8192], P(('group', 'wide'), 'tensor'), parts along dimension 0, may hold values from -6 to 6
- gain: float32 [16384], P('group'), parts along dimension 0, may hold values from 0.5 to 2
- gate_weight: bfloat16 [16384, 16384], P(('group', 'wide', 'tensor')), parts along dimension 0, may hold values from -0.09375 to 0.09375
- up_weight: bfloat16 [16384, 16384], P(('group', 'wide', 'tensor')), parts along dimension 0, may hold values from -0.09375 to 0.09375
- gate_mask: int32 [256, 256], P('group'), parts along dimension 0, may hold values from 0 to 1, as said below
- up_mask: int32 [256, 256], P('group'), parts along dimension 0, may hold values from 0 to 1, as said below
Outputs:
- hidden: bfloat16 [512, 16384], P(('group', 'wide'), 'tensor'), parts along dimension 0
The draws below stay inside these ranges and needn't reach their ends.
There are 2 independent parts, one for each index of `group`. The reference program is written for one: setup_inputs(seed, part) draws one part's arguments, and reference() takes and returns one part's arrays. A program takes and returns all parts, laid end to end along the dimension named above; each array names one. Nothing has to cross between parts.
Inputs may be any that keep to these rules, and one draw needn't show every extreme that they name: `gate_mask`: A 1 keeps a block, a 0 prunes it; the share of kept blocks differs between groups of consecutive hidden-unit blocks. `up_mask`: as for gate_mask.
All inputs are finite; a program needn't handle non-finite values.
Results may differ from the reference program's by a relative error of at most 0.0058.
Values may be sent and summed in bfloat16 or wider, within the bound.
A program may use at most 256 MiB of HBM per device.

```python
import math
import jax
import jax.numpy as jnp
from jax import lax

D = 8192
FF = 16384
BS = 64
TOKENS = 256
N_TENSOR = 8


def mask_draw(key, rows, cols, groups):
    first = jax.random.fold_in(key, 11)
    second = jax.random.fold_in(key, 23)
    levels = jax.random.randint(first, (groups,), 1, 4)
    limits = jnp.repeat(levels, cols // groups)[None, :]
    draws = jax.random.randint(second, (rows, cols), 0, 4)
    return (draws < limits).astype(jnp.int32)


def draw_gate_mask(key, part):
    return mask_draw(jax.random.fold_in(key, 1), D // BS, FF // BS, N_TENSOR)


def draw_up_mask(key, part):
    return mask_draw(jax.random.fold_in(key, 2), D // BS, FF // BS, N_TENSOR)


def steps_of(own_key, dims, shards, low, top_value):
    level = 1.0
    for axis_at, blocks in shards:
        heights = jax.random.uniform(jax.random.fold_in(jax.random.fold_in(own_key, 6), axis_at), (blocks,), jnp.float32, low / len(shards), top_value / len(shards))
        level = level * jnp.repeat(jnp.exp(heights), dims[axis_at] // blocks).reshape((-1,) + (1,) * (len(dims) - 1 - axis_at))
    return level


def normal_values(rng, dims, scale, limit, pieces=(), held_as=jnp.bfloat16):
    entries = scale * jax.random.normal(rng, dims, jnp.float32)
    if pieces:
        entries = entries * steps_of(rng, dims, pieces, -0.22, 0.18)
    return jnp.clip(entries, -limit, limit).astype(held_as)


def setup_inputs(seed: int = 0, part: int = 0) -> dict:
    seeds = jax.random.split(jax.random.key(seed), 7)
    own_keys = jax.random.split(jax.random.fold_in(seeds[6], part), 7)
    return {
        "tokens": normal_values(own_keys[0], (TOKENS, D), 1.0, 6.0, ((0, 2), (1, 8))),
        "gain": jnp.clip(jnp.exp(jax.random.uniform(own_keys[1], (D,), jnp.float32, math.log(0.5), math.log(2.0))), 0.5, 2.0),
        "gate_weight": normal_values(own_keys[2], (D, FF), (D // 2) ** -0.5, 0.09375, ((0, 16),)),
        "up_weight": normal_values(own_keys[3], (D, FF), (D // 2) ** -0.5, 0.09375, ((0, 16),)),
        "gate_mask": draw_gate_mask(jax.random.fold_in(jax.random.fold_in(seeds[6], part), 71), part),
        "up_mask": draw_up_mask(jax.random.fold_in(jax.random.fold_in(seeds[6], part), 71), part),
    }


def expand(mask, weight):
    rows, cols = mask.shape
    blocks = weight.reshape(rows, BS, cols, BS) * mask.astype(jnp.bfloat16)[:, None, :, None]
    return blocks.reshape(weight.shape)

def reference(tokens, gain, gate_weight, up_weight, gate_mask, up_mask):
    values = tokens.astype(jnp.float32)
    scale = lax.rsqrt(lax.optimization_barrier(jnp.mean(values * values, axis=-1, keepdims=True)) + 1e-05)
    normed = (values * scale * gain).astype(jnp.bfloat16)
    gate = jnp.dot(normed, expand(gate_mask, gate_weight), preferred_element_type=jnp.float32)
    up = jnp.dot(normed, expand(up_mask, up_weight), preferred_element_type=jnp.float32)
    return (jax.nn.silu(gate) * up).astype(jnp.bfloat16)
```

```python
import functools

import jax
import jax.numpy as jnp
from jax import lax
from jax.experimental import pallas as pl
from jax.experimental.pallas import tpu as pltpu
from jax.sharding import PartitionSpec as P

BS = 64
SUB = 512
LAG = 6
W_SLOTS = 4
X_SLOTS = 4
EPS = 1e-05
MESH = pl.DeviceIdType.MESH


def kernel(
    nt, ny, sub, tok_ref, gain_ref, gw_hbm, uw_hbm, gm_ref, um_ref, out_ref,
    stats, stat_out, xbuf, xs, mexp, wbuf, own, xsend, xrecv, ysend, yrecv, zsend, zrecv,
    stat_ssem, stat_rsem, tok_ssem, tok_rsem, wsem, x_ssem, x_rsem, y_ssem, y_rsem, z_ssem, z_rsem,
):
    nz = nt // ny
    w = lax.axis_index("wide")
    t = lax.axis_index("tensor")
    z, y = lax.div(t, ny), lax.rem(t, ny)
    me = w * nt + t
    peers = 2 * nt
    rows, feats = tok_ref.shape
    depth, ff = gw_hbm.shape
    width = ff // nt
    per = width // sub
    pairs = nz * per
    units = 2 * pairs
    blocks = depth // BS

    def at(dev):
        return {"wide": lax.div(dev, nt), "tensor": lax.rem(dev, nt)}

    def z_of(pair):
        k = lax.div(pair, per)
        right, left = nz - 1 - z, z
        both = jnp.minimum(right, left)
        paired = k < 2 * both
        idx = jnp.where(paired, lax.div(k, 2), k - both)
        is_right = jnp.where(paired, lax.rem(k, 2) == 0, right > left)
        dest = jnp.where(is_right, nz - 1 - idx, idx)
        return jnp.where(k == nz - 1, z, dest)

    def column(unit):
        pair, kind = lax.div(unit, 2), lax.rem(unit, 2)
        y_to = jnp.where(kind == 0, ny - 1 - y, y)
        owner = z_of(pair) * ny + y_to
        return pl.multiple_of(owner * width + lax.rem(pair, per) * sub, 128)

    def weight_copies(unit):
        slot = lax.rem(unit, W_SLOTS)
        cols = pl.ds(column(unit), sub)
        return (
            pltpu.make_async_copy(gw_hbm.at[:, cols], wbuf.at[slot, 0], wsem.at[slot, 0]),
            pltpu.make_async_copy(uw_hbm.at[:, cols], wbuf.at[slot, 1], wsem.at[slot, 1]),
        )

    def fetch(unit):
        for copy in weight_copies(unit):
            copy.start()

    for unit in range(min(W_SLOTS, units)):
        fetch(jnp.int32(unit))

    barrier = pltpu.get_barrier_semaphore()

    @pl.loop(1, peers)
    def _(d):
        pl.semaphore_signal(
            barrier, inc=1, device_id=at(lax.rem(me + d, peers)), device_id_type=MESH
        )

    total = jnp.zeros((rows, 128), jnp.float32)
    for f in range(0, feats, 128):
        v = tok_ref[:, f:f + 128].astype(jnp.float32)
        total = total + v * v
    line = jnp.sum(total.T, axis=0, keepdims=True)
    stat_out[...] = jnp.broadcast_to(line, (8, rows))
    stats[me] = jnp.broadcast_to(line, (8, rows))

    pl.semaphore_wait(barrier, peers - 1)

    def token_copy(h):
        dev = 2 * t + h
        return dev, pltpu.make_async_remote_copy(
            src_ref=tok_ref.at[:, h * depth:(h + 1) * depth],
            dst_ref=xbuf.at[w],
            send_sem=tok_ssem.at[h],
            recv_sem=tok_rsem.at[w],
            device_id=at(dev),
            device_id_type=MESH,
        )

    for h in range(2):
        dev, copy = token_copy(h)

        @pl.when(dev != me)
        def _():
            copy.start()

        @pl.when(dev == me)
        def _():
            xbuf[w] = tok_ref[:, h * depth:(h + 1) * depth]

    def stat_copy(d, src):
        return pltpu.make_async_remote_copy(
            src_ref=stat_out,
            dst_ref=stats.at[src],
            send_sem=stat_ssem.at[d],
            recv_sem=stat_rsem.at[src],
            device_id=at(lax.rem(me + d, peers)),
            device_id_type=MESH,
        )

    @pl.loop(1, peers)
    def _(d):
        stat_copy(d, me).start()

    mrows = gm_ref.shape[0]
    pick = (
        lax.broadcasted_iota(jnp.int32, (8, mrows), 1)
        == lax.broadcasted_iota(jnp.int32, (8, mrows), 0) + me * blocks
    ).astype(jnp.float32).astype(jnp.bfloat16)
    mine = []
    for m_ref in (gm_ref, um_ref):
        kept = m_ref[...].astype(jnp.float32).astype(jnp.bfloat16)
        mine.append(
            jnp.dot(pick, kept, preferred_element_type=jnp.float32).astype(jnp.bfloat16)
        )
    mcols = gm_ref.shape[1]

    @pl.loop(0, ff // sub)
    def _(n):
        first = lax.broadcasted_iota(jnp.int32, (mcols, sub), 0) * BS - n * sub
        col = lax.broadcasted_iota(jnp.int32, (mcols, sub), 1)
        spread = ((col >= first) & (col < first + BS)).astype(jnp.float32).astype(jnp.bfloat16)
        for a in range(2):
            mexp[a, :, pl.ds(pl.multiple_of(n * sub, 128), sub)] = jnp.dot(
                mine[a], spread, preferred_element_type=jnp.float32
            )

    @pl.loop(1, peers)
    def _(d):
        stat_copy(d, lax.rem(me + d, peers)).wait_recv()

    for v in range(2):
        @pl.when(v * nt + lax.div(me, 2) != me)
        def _():
            pltpu.make_async_remote_copy(
                src_ref=tok_ref.at[:, 0:depth], dst_ref=xbuf.at[v],
                send_sem=tok_ssem.at[0], recv_sem=tok_rsem.at[v],
                device_id=at(lax.rem(me + 1, peers)), device_id_type=MESH,
            ).wait_recv()

    gain = gain_ref[:, pl.ds(pl.multiple_of(me * depth, 128), depth)]
    for half in range(2):
        v = w if half == 0 else 1 - w
        ssq = jnp.sum(stats[pl.ds(v * nt, nt)], axis=0)[0:1, :]
        scale = lax.rsqrt(ssq / (feats * nt) + EPS)
        scale = jnp.broadcast_to(scale, (rows, rows)).T[:, 0:1]
        xs[half * rows:(half + 1) * rows, :] = (
            xbuf[v].astype(jnp.float32) * scale * gain
        ).astype(jnp.bfloat16)

    def x_copy(unit):
        slot = lax.rem(unit, X_SLOTS)
        return pltpu.make_async_remote_copy(
            src_ref=xsend.at[slot], dst_ref=xrecv.at[unit],
            send_sem=x_ssem.at[slot], recv_sem=x_rsem.at[unit],
            device_id={"wide": 1 - w}, device_id_type=MESH,
        )

    def y_copy(pair):
        return pltpu.make_async_remote_copy(
            src_ref=ysend.at[pair], dst_ref=yrecv.at[pair],
            send_sem=y_ssem.at[pair], recv_sem=y_rsem.at[pair],
            device_id={"tensor": z * ny + (ny - 1 - y)}, device_id_type=MESH,
        )

    def z_copy(pair, side, piece, z_to):
        return pltpu.make_async_remote_copy(
            src_ref=zsend.at[pair], dst_ref=zrecv.at[side, piece],
            send_sem=z_ssem.at[pair], recv_sem=z_rsem.at[side, piece],
            device_id={"tensor": z_to * ny + y}, device_id_type=MESH,
        )

    def compute(unit):
        slot = lax.rem(unit, W_SLOTS)
        xslot = lax.rem(unit, X_SLOTS)
        cols = pl.ds(column(unit), sub)
        for copy in weight_copies(unit):
            copy.wait()

        @pl.when(unit >= X_SLOTS)
        def _():
            x_copy(unit - X_SLOTS).wait_send()

        for a in range(2):
            kept = []
            for r in range(blocks):
                keep = jnp.broadcast_to(mexp[a, r:r + 1, cols], (BS, sub)).astype(jnp.bfloat16)
                kept.append(wbuf[slot, a, r * BS:(r + 1) * BS, :] * keep)
            part = jnp.dot(
                xs[...], jnp.concatenate(kept, axis=0), preferred_element_type=jnp.float32
            )
            own[xslot, :, a * sub:(a + 1) * sub] = part[:rows]
            xsend[xslot, :, a * sub:(a + 1) * sub] = part[rows:]
        x_copy(unit).start()

        @pl.when(unit + W_SLOTS < units)
        def _():
            fetch(unit + W_SLOTS)

    def finish(unit, kind):
        pair = lax.div(unit, 2)
        x_copy(unit).wait_recv()
        both = own[lax.rem(unit, X_SLOTS)] + xrecv[unit]
        if kind == 0:
            ysend[pair] = both.astype(jnp.bfloat16)
            y_copy(pair).start()
        else:
            xrecv[unit] = both

    def settle(pair):
        unit = 2 * pair + 1
        dest = z_of(pair)
        piece = dest * per + lax.rem(pair, per)
        y_copy(pair).wait_recv()
        xrecv[unit] = xrecv[unit] + yrecv[pair].astype(jnp.float32)

        @pl.when((dest >= z) & (z > 0))
        def _():
            z_copy(pair, 0, piece, z - 1).wait_recv()
            xrecv[unit] = xrecv[unit] + zrecv[0, piece].astype(jnp.float32)

        @pl.when((dest <= z) & (z < nz - 1))
        def _():
            z_copy(pair, 1, piece, z + 1).wait_recv()
            xrecv[unit] = xrecv[unit] + zrecv[1, piece].astype(jnp.float32)

        @pl.when(dest != z)
        def _():
            zsend[pair] = xrecv[unit].astype(jnp.bfloat16)

        @pl.when(dest > z)
        def _():
            z_copy(pair, 0, piece, z + 1).start()

        @pl.when(dest < z)
        def _():
            z_copy(pair, 1, piece, z - 1).start()

        @pl.when(dest == z)
        def _():
            g = xrecv[unit, :, 0:sub]
            u = xrecv[unit, :, sub:2 * sub]
            at_col = pl.multiple_of(lax.rem(pair, per) * sub, 128)
            out_ref[:, pl.ds(at_col, sub)] = (g / (1.0 + jnp.exp(-g)) * u).astype(out_ref.dtype)

    @pl.loop(0, pairs + LAG)
    def _(i):
        @pl.when(i < pairs)
        def _():
            compute(2 * i)

        @pl.when((i >= 1) & (i <= pairs))
        def _():
            finish(2 * i - 1, 1)

        @pl.when(i < pairs)
        def _():
            compute(2 * i + 1)
            finish(2 * i, 0)

        @pl.when(i >= LAG)
        def _():
            settle(i - LAG)

    for unit in range(max(0, units - X_SLOTS), units):
        x_copy(jnp.int32(unit)).wait_send()

    @pl.loop(0, pairs)
    def _(pair):
        y_copy(pair).wait_send()

        @pl.when(z_of(pair) != z)
        def _():
            z_copy(pair, 0, pair, lax.rem(z + 1, nz)).wait_send()

    @pl.loop(1, peers)
    def _(d):
        stat_copy(d, me).wait_send()

    for h in range(2):
        dev, copy = token_copy(h)

        @pl.when(dev != me)
        def _():
            copy.wait_send()


def local(tokens, gain, gate_weight, up_weight, gate_mask, up_mask):
    nt = lax.axis_size("tensor")
    ny = 2
    rows, feats = tokens.shape
    depth, ff = gate_weight.shape
    width = ff // nt
    sub = min(SUB, width)
    pairs = (nt // ny) * (width // sub)
    peers = 2 * nt
    dma = pltpu.SemaphoreType.DMA
    vmem = pl.BlockSpec(memory_space=pltpu.VMEM)
    hbm = pl.BlockSpec(memory_space=pl.ANY)
    tile = (rows, 2 * sub)
    return pl.pallas_call(
        functools.partial(kernel, nt, ny, sub),
        out_shape=jax.ShapeDtypeStruct((rows, width), jnp.bfloat16),
        in_specs=[vmem, vmem, hbm, hbm, vmem, vmem],
        out_specs=vmem,
        scratch_shapes=[
            pltpu.VMEM((peers, 8, rows), jnp.float32),
            pltpu.VMEM((8, rows), jnp.float32),
            pltpu.VMEM((2, rows, depth), jnp.bfloat16),
            pltpu.VMEM((2 * rows, depth), jnp.bfloat16),
            pltpu.VMEM((2, 8, ff), jnp.float32),
            pltpu.VMEM((W_SLOTS, 2, depth, sub), jnp.bfloat16),
            pltpu.VMEM((X_SLOTS,) + tile, jnp.float32),
            pltpu.VMEM((X_SLOTS,) + tile, jnp.float32),
            pltpu.VMEM((2 * pairs,) + tile, jnp.float32),
            pltpu.VMEM((pairs,) + tile, jnp.bfloat16),
            pltpu.VMEM((pairs,) + tile, jnp.bfloat16),
            pltpu.VMEM((pairs,) + tile, jnp.bfloat16),
            pltpu.VMEM((2, pairs) + tile, jnp.bfloat16),
            dma((peers,)), dma((peers,)), dma((2,)), dma((2,)), dma((W_SLOTS, 2)),
            dma((X_SLOTS,)), dma((2 * pairs,)), dma((pairs,)), dma((pairs,)),
            dma((pairs,)), dma((2, pairs)),
        ],
        compiler_params=pltpu.CompilerParams(
            collective_id=0, has_side_effects=True, vmem_limit_bytes=60 * 1024 * 1024
        ),
    )(tokens, gain.reshape(1, -1), gate_weight, up_weight, gate_mask, up_mask)


def solution(mesh):
    in_specs = (
        P(("group", "wide"), "tensor"),
        P("group"),
        P(("group", "wide", "tensor"), None),
        P(("group", "wide", "tensor"), None),
        P("group", None),
        P("group", None),
    )
    out_specs = P(("group", "wide"), "tensor")
    return jax.shard_map(local, mesh=mesh, in_specs=in_specs, out_specs=out_specs, check_vma=False)
```

```python
import functools

import jax
import jax.numpy as jnp
from jax import lax
from jax.experimental import pallas as pl
from jax.experimental.pallas import tpu as pltpu
from jax.sharding import PartitionSpec as P

BS = 64
SUB = 512
LAG = 6
W_SLOTS = 4
X_SLOTS = 4
EPS = 1e-05
MESH = pl.DeviceIdType.MESH


def kernel(
    nt, ny, sub, tok_ref, gain_ref, gw_hbm, uw_hbm, gm_ref, um_ref, out_ref,
    stats, stat_out, xbuf, xs, mine, wbuf, own, xsend, xrecv, ysend, yrecv, zsend, zrecv,
    stat_ssem, stat_rsem, tok_ssem, tok_rsem, wsem, x_ssem, x_rsem, y_ssem, y_rsem, z_ssem, z_rsem,
):
    nz = nt // ny
    w = lax.axis_index("wide")
    t = lax.axis_index("tensor")
    z, y = lax.div(t, ny), lax.rem(t, ny)
    me = w * nt + t
    peers = 2 * nt
    rows, feats = tok_ref.shape
    depth, ff = gw_hbm.shape
    width = ff // nt
    per = width // sub
    pairs = nz * per
    units = 2 * pairs
    blocks = depth // BS

    def at(dev):
        return {"wide": lax.div(dev, nt), "tensor": lax.rem(dev, nt)}

    def z_of(pair):
        k = lax.div(pair, per)
        right, left = nz - 1 - z, z
        both = jnp.minimum(right, left)
        paired = k < 2 * both
        idx = jnp.where(paired, lax.div(k, 2), k - both)
        is_right = jnp.where(paired, (lax.rem(k, 2) == 0) == (right > left), right > left)
        dest = jnp.where(is_right, nz - 1 - idx, idx)
        return jnp.where(k == nz - 1, z, dest)

    def column(unit):
        pair, kind = lax.div(unit, 2), lax.rem(unit, 2)
        y_to = jnp.where(kind == 0, ny - 1 - y, y)
        owner = z_of(pair) * ny + y_to
        return pl.multiple_of(owner * width + lax.rem(pair, per) * sub, 128)

    def weight_copies(unit):
        slot = lax.rem(unit, W_SLOTS)
        cols = pl.ds(column(unit), sub)
        return (
            pltpu.make_async_copy(gw_hbm.at[:, cols], wbuf.at[slot, 0], wsem.at[slot, 0]),
            pltpu.make_async_copy(uw_hbm.at[:, cols], wbuf.at[slot, 1], wsem.at[slot, 1]),
        )

    def fetch(unit):
        for copy in weight_copies(unit):
            copy.start()

    for unit in range(min(W_SLOTS, units)):
        fetch(jnp.int32(unit))

    barrier = pltpu.get_barrier_semaphore()

    @pl.loop(1, peers)
    def _(d):
        pl.semaphore_signal(
            barrier, inc=1, device_id=at(lax.rem(me + d, peers)), device_id_type=MESH
        )

    total = jnp.zeros((rows, 128), jnp.float32)
    for f in range(0, feats, 128):
        v = tok_ref[:, f:f + 128].astype(jnp.float32)
        total = total + v * v
    line = jnp.sum(total.T, axis=0, keepdims=True)
    stat_out[...] = jnp.broadcast_to(line, (8, rows))
    stats[me] = jnp.broadcast_to(line, (8, rows))

    pl.semaphore_wait(barrier, peers - 1)

    def token_copy(h):
        dev = 2 * t + h
        return dev, pltpu.make_async_remote_copy(
            src_ref=tok_ref.at[:, h * depth:(h + 1) * depth],
            dst_ref=xbuf.at[w],
            send_sem=tok_ssem.at[h],
            recv_sem=tok_rsem.at[w],
            device_id=at(dev),
            device_id_type=MESH,
        )

    for h in range(2):
        dev, copy = token_copy(h)

        @pl.when(dev != me)
        def _():
            copy.start()

        @pl.when(dev == me)
        def _():
            xbuf[w] = tok_ref[:, h * depth:(h + 1) * depth]

    def stat_copy(d, src):
        return pltpu.make_async_remote_copy(
            src_ref=stat_out,
            dst_ref=stats.at[src],
            send_sem=stat_ssem.at[d],
            recv_sem=stat_rsem.at[src],
            device_id=at(lax.rem(me + d, peers)),
            device_id_type=MESH,
        )

    @pl.loop(1, peers)
    def _(d):
        stat_copy(d, me).start()

    mrows = gm_ref.shape[0]
    pick = (
        lax.broadcasted_iota(jnp.int32, (8, mrows), 1)
        == lax.broadcasted_iota(jnp.int32, (8, mrows), 0) + me * blocks
    ).astype(jnp.float32).astype(jnp.bfloat16)
    for a, m_ref in enumerate((gm_ref, um_ref)):
        kept = m_ref[...].astype(jnp.float32).astype(jnp.bfloat16)
        mine[a * 8:(a + 1) * 8, :] = jnp.dot(pick, kept, preferred_element_type=jnp.float32)
    mcols = gm_ref.shape[1]

    @pl.loop(1, peers)
    def _(d):
        stat_copy(d, lax.rem(me + d, peers)).wait_recv()

    for v in range(2):
        @pl.when(v * nt + lax.div(me, 2) != me)
        def _():
            pltpu.make_async_remote_copy(
                src_ref=tok_ref.at[:, 0:depth], dst_ref=xbuf.at[v],
                send_sem=tok_ssem.at[0], recv_sem=tok_rsem.at[v],
                device_id=at(lax.rem(me + 1, peers)), device_id_type=MESH,
            ).wait_recv()

    gain = gain_ref[:, pl.ds(pl.multiple_of(me * depth, 128), depth)]
    for half in range(2):
        v = w if half == 0 else 1 - w
        ssq = jnp.sum(stats[pl.ds(v * nt, nt)], axis=0)[0:1, :]
        scale = lax.rsqrt(ssq / (feats * nt) + EPS)
        scale = jnp.broadcast_to(scale, (rows, rows)).T[:, 0:1]
        xs[half * rows:(half + 1) * rows, :] = (
            xbuf[v].astype(jnp.float32) * scale * gain
        ).astype(jnp.bfloat16)

    def x_copy(unit):
        slot = lax.rem(unit, X_SLOTS)
        return pltpu.make_async_remote_copy(
            src_ref=xsend.at[slot], dst_ref=xrecv.at[unit],
            send_sem=x_ssem.at[slot], recv_sem=x_rsem.at[unit],
            device_id={"wide": 1 - w}, device_id_type=MESH,
        )

    def y_copy(pair):
        return pltpu.make_async_remote_copy(
            src_ref=ysend.at[pair], dst_ref=yrecv.at[pair],
            send_sem=y_ssem.at[pair], recv_sem=y_rsem.at[pair],
            device_id={"tensor": z * ny + (ny - 1 - y)}, device_id_type=MESH,
        )

    def z_copy(pair, side, piece, z_to):
        return pltpu.make_async_remote_copy(
            src_ref=zsend.at[pair], dst_ref=zrecv.at[side, piece],
            send_sem=z_ssem.at[pair], recv_sem=z_rsem.at[side, piece],
            device_id={"tensor": z_to * ny + y}, device_id_type=MESH,
        )

    def compute(unit):
        slot = lax.rem(unit, W_SLOTS)
        xslot = lax.rem(unit, X_SLOTS)
        first = lax.broadcasted_iota(jnp.int32, (mcols, sub), 0) * BS - column(unit)
        col = lax.broadcasted_iota(jnp.int32, (mcols, sub), 1)
        spread = ((col >= first) & (col < first + BS)).astype(jnp.float32).astype(jnp.bfloat16)
        mexp = jnp.dot(mine[...].astype(jnp.bfloat16), spread, preferred_element_type=jnp.float32)
        for copy in weight_copies(unit):
            copy.wait()

        @pl.when(unit >= X_SLOTS)
        def _():
            x_copy(unit - X_SLOTS).wait_send()

        for a in range(2):
            kept = []
            for r in range(blocks):
                keep = jnp.broadcast_to(mexp[a * 8 + r:a * 8 + r + 1, :], (BS, sub)).astype(jnp.bfloat16)
                kept.append(wbuf[slot, a, r * BS:(r + 1) * BS, :] * keep)
            part = jnp.dot(
                xs[...], jnp.concatenate(kept, axis=0), preferred_element_type=jnp.float32
            )
            own[xslot, :, a * sub:(a + 1) * sub] = part[:rows]
            xsend[xslot, :, a * sub:(a + 1) * sub] = part[rows:]
        x_copy(unit).start()

        @pl.when(unit + W_SLOTS < units)
        def _():
            fetch(unit + W_SLOTS)

    def finish(unit, kind):
        pair = lax.div(unit, 2)
        x_copy(unit).wait_recv()
        both = own[lax.rem(unit, X_SLOTS)] + xrecv[unit]
        if kind == 0:
            ysend[pair] = both.astype(jnp.bfloat16)
            y_copy(pair).start()
        else:
            xrecv[unit] = both

    def settle(pair):
        unit = 2 * pair + 1
        dest = z_of(pair)
        piece = dest * per + lax.rem(pair, per)
        y_copy(pair).wait_recv()
        xrecv[unit] = xrecv[unit] + yrecv[pair].astype(jnp.float32)

        @pl.when((dest >= z) & (z > 0))
        def _():
            z_copy(pair, 0, piece, z - 1).wait_recv()
            xrecv[unit] = xrecv[unit] + zrecv[0, piece].astype(jnp.float32)

        @pl.when((dest <= z) & (z < nz - 1))
        def _():
            z_copy(pair, 1, piece, z + 1).wait_recv()
            xrecv[unit] = xrecv[unit] + zrecv[1, piece].astype(jnp.float32)

        @pl.when(dest != z)
        def _():
            zsend[pair] = xrecv[unit].astype(jnp.bfloat16)

        @pl.when(dest > z)
        def _():
            z_copy(pair, 0, piece, z + 1).start()

        @pl.when(dest < z)
        def _():
            z_copy(pair, 1, piece, z - 1).start()

        @pl.when(dest == z)
        def _():
            g = xrecv[unit, :, 0:sub]
            u = xrecv[unit, :, sub:2 * sub]
            at_col = pl.multiple_of(lax.rem(pair, per) * sub, 128)
            out_ref[:, pl.ds(at_col, sub)] = (g / (1.0 + jnp.exp(-g)) * u).astype(out_ref.dtype)

    @pl.loop(0, pairs + LAG)
    def _(i):
        @pl.when(i < pairs)
        def _():
            compute(2 * i)

        @pl.when((i >= 1) & (i <= pairs))
        def _():
            finish(2 * i - 1, 1)

        @pl.when(i < pairs)
        def _():
            finish(2 * i, 0)
            compute(2 * i + 1)

        @pl.when(i >= LAG)
        def _():
            settle(i - LAG)

    for unit in range(max(0, units - X_SLOTS), units):
        x_copy(jnp.int32(unit)).wait_send()

    @pl.loop(0, pairs)
    def _(pair):
        y_copy(pair).wait_send()

        @pl.when(z_of(pair) != z)
        def _():
            z_copy(pair, 0, pair, lax.rem(z + 1, nz)).wait_send()

    @pl.loop(1, peers)
    def _(d):
        stat_copy(d, me).wait_send()

    for h in range(2):
        dev, copy = token_copy(h)

        @pl.when(dev != me)
        def _():
            copy.wait_send()


def local(tokens, gain, gate_weight, up_weight, gate_mask, up_mask):
    nt = lax.axis_size("tensor")
    ny = 2
    rows, feats = tokens.shape
    depth, ff = gate_weight.shape
    width = ff // nt
    sub = min(SUB, width)
    pairs = (nt // ny) * (width // sub)
    peers = 2 * nt
    dma = pltpu.SemaphoreType.DMA
    vmem = pl.BlockSpec(memory_space=pltpu.VMEM)
    hbm = pl.BlockSpec(memory_space=pl.ANY)
    tile = (rows, 2 * sub)
    return pl.pallas_call(
        functools.partial(kernel, nt, ny, sub),
        out_shape=jax.ShapeDtypeStruct((rows, width), jnp.bfloat16),
        in_specs=[vmem, vmem, hbm, hbm, vmem, vmem],
        out_specs=vmem,
        scratch_shapes=[
            pltpu.VMEM((peers, 8, rows), jnp.float32),
            pltpu.VMEM((8, rows), jnp.float32),
            pltpu.VMEM((2, rows, depth), jnp.bfloat16),
            pltpu.VMEM((2 * rows, depth), jnp.bfloat16),
            pltpu.VMEM((16, gate_mask.shape[1]), jnp.float32),
            pltpu.VMEM((W_SLOTS, 2, depth, sub), jnp.bfloat16),
            pltpu.VMEM((X_SLOTS,) + tile, jnp.float32),
            pltpu.VMEM((X_SLOTS,) + tile, jnp.float32),
            pltpu.VMEM((2 * pairs,) + tile, jnp.float32),
            pltpu.VMEM((pairs,) + tile, jnp.bfloat16),
            pltpu.VMEM((pairs,) + tile, jnp.bfloat16),
            pltpu.VMEM((pairs,) + tile, jnp.bfloat16),
            pltpu.VMEM((2, pairs) + tile, jnp.bfloat16),
            dma((peers,)), dma((peers,)), dma((2,)), dma((2,)), dma((W_SLOTS, 2)),
            dma((X_SLOTS,)), dma((2 * pairs,)), dma((pairs,)), dma((pairs,)),
            dma((pairs,)), dma((2, pairs)),
        ],
        compiler_params=pltpu.CompilerParams(
            collective_id=0, has_side_effects=True, vmem_limit_bytes=60 * 1024 * 1024
        ),
    )(tokens, gain.reshape(1, -1), gate_weight, up_weight, gate_mask, up_mask)


def solution(mesh):
    in_specs = (
        P(("group", "wide"), "tensor"),
        P("group"),
        P(("group", "wide", "tensor"), None),
        P(("group", "wide", "tensor"), None),
        P("group", None),
        P("group", None),
    )
    out_specs = P(("group", "wide"), "tensor")
    return jax.shard_map(local, mesh=mesh, in_specs=in_specs, out_specs=out_specs, check_vma=False)
```
